32 devices in a mesh: sec: 8 (over z, y), tile: 4 (over x, core).
Axes of the slice: x: 2, y: 2, z: 4, core: 2. Of those that a mesh axis runs over, the one named last changes fastest.
Arguments:
- image: bfloat16 [8, 1024, 1024], P('sec', 'tile'), may hold values from -6 to 6
- weight: bfloat16 [8, 1024, 1024], P('sec', 'tile'), may hold values from 0.25 to 4
- lens_filter_taps: float32 [8, 4, 25], P('sec', 'tile'), may hold values from -2 to 2
- block_src: int32 [8, 4, 4, 2], P('sec', 'tile'), may hold values from 0 to 15
- block_dst: int32 [8, 4, 4, 2], P('sec', None, 'tile'), may hold values from 0 to 3, as said below
- valid_count: int32 [8, 4, 4], P('sec', 'tile'), may hold values from 1 to 2, as said below
- anchor: bfloat16 [16, 128, 128], P('tile'), may hold values from -6 to 6
Outputs:
- correlation: float32 [8, 32, 128, 128], P('sec', 'tile')
The draws below stay inside these ranges and needn't reach their ends.
Inputs may be any that keep to these rules, and one draw needn't show every extreme that they name: `block_dst`: every block of every strip receives at least one live slot. `valid_count`: in every section some strip receives 2 live slots from every tile; block_src and block_dst are 0 in slots at or beyond the valid count.
All inputs are finite; a program needn't handle non-finite values.
Results may differ from the reference program's by a relative error of at most 0.02.
Values may be sent and summed in bfloat16 or wider, within the bound.
A program may use at most 64 MiB of HBM per device.

```python
import math
import jax
import jax.numpy as jnp
from jax import lax

B = 128
CAP = 2
TH = 256
TW = 1024
TB = 16
SB = 4
SECTION_COUNT = 8
TILES = 4
ROWS = 1024


def placement_lists(key):
    pieces = jax.random.split(jax.random.fold_in(key, 7), 5)
    counts = jax.random.randint(pieces[0], (SECTION_COUNT, TILES, TILES), 1, CAP + 1)
    hot_strip = jax.random.randint(pieces[1], (SECTION_COUNT,), 0, TILES)
    is_hot = jnp.arange(TILES)[None, None, :] == hot_strip[:, None, None]
    counts = jnp.where(is_hot, CAP, counts).astype(jnp.int32)
    source_ids = jax.random.randint(pieces[2], (SECTION_COUNT, TILES, TILES, CAP), 0, TB)
    dest_ids = jax.random.randint(pieces[3], (SECTION_COUNT, TILES, TILES, CAP), 0, SB)
    offsets = jax.random.randint(pieces[4], (SECTION_COUNT,), 0, SB)
    tile_index = jnp.arange(TILES, dtype=jnp.int32)
    first_dest = (tile_index[None, :, None] + tile_index[None, None, :] + offsets[:, None, None]) % SB
    is_first = jnp.arange(CAP)[None, None, None, :] == 0
    dest_ids = jnp.where(is_first, first_dest[..., None], dest_ids)
    is_live = jnp.arange(CAP)[None, None, None, :] < counts[..., None]
    source_ids = jnp.where(is_live, source_ids, 0).astype(jnp.int32)
    dest_ids = jnp.where(is_live, dest_ids, 0).astype(jnp.int32)
    return (source_ids, dest_ids, counts)


def draw_block_src(key, part):
    return placement_lists(key)[0]


def draw_block_dst(key, part):
    return placement_lists(key)[1]


def draw_valid_count(key, part):
    return placement_lists(key)[2]


def steps_of(rng, dims, cuts, smallest, largest):
    def one(axis_at, blocks):
        draws = jax.random.uniform(jax.random.fold_in(jax.random.fold_in(rng, 6), axis_at), (blocks,), jnp.float32, smallest / len(cuts), largest / len(cuts))
        return jnp.repeat(jnp.exp(draws), dims[axis_at] // blocks).reshape((-1,) + (1,) * (len(dims) - axis_at - 1))

    factor_of = one(*cuts[0])
    for cut in cuts[1:]:
        factor_of = factor_of * one(*cut)
    return factor_of


def normal_values(stream_key, dims, width, most, cuts=(), kind=jnp.bfloat16):
    values = width * jax.random.normal(stream_key, dims, jnp.float32)
    if cuts:
        values = values * steps_of(stream_key, dims, cuts, -0.22, 0.18)
    return jnp.clip(values, -most, most).astype(kind)


def setup_inputs(seed: int = 0) -> dict:
    key_list = jax.random.split(jax.random.key(seed), 8)
    return {
        "image": normal_values(key_list[0], (SECTION_COUNT, ROWS, TW), 1.0, 6.0, ((0, 8), (1, 4))),
        "weight": jnp.clip(jnp.exp(math.log(4.0) - 2.7725887 * jax.random.uniform(key_list[1], (SECTION_COUNT, ROWS, TW), jnp.float32) ** steps_of(key_list[1], (SECTION_COUNT, ROWS, TW), ((0, 8), (1, 4)), -0.2, 0.2)), 0.25, 4.0).astype(jnp.bfloat16),
        "lens_filter_taps": normal_values(key_list[2], (SECTION_COUNT, TILES, 25), 0.4, 2.0, ((0, 8), (1, 4)), jnp.float32),
        "block_src": draw_block_src(jax.random.fold_in(key_list[7], 71), 0),
        "block_dst": draw_block_dst(jax.random.fold_in(key_list[7], 71), 0),
        "valid_count": draw_valid_count(jax.random.fold_in(key_list[7], 71), 0),
        "anchor": normal_values(key_list[6], (TILES * SB, B, B), 1.0, 6.0, ((0, 4),)),
    }


def render_section(operands):
    section_image, section_weight, kernel_taps, source_ids, dest_ids, counts = operands
    rows_total = section_image.shape[0]
    padded = jnp.pad(section_image, 2)
    row_taps = jnp.repeat(kernel_taps, TH, axis=0)
    corrected = jnp.zeros((rows_total, TW), jnp.float32)
    for row_off in range(5):
        for col_off in range(5):
            corrected = corrected + row_taps[:, row_off * 5 + col_off][:, None] * padded[row_off:row_off + rows_total, col_off:col_off + TW].astype(jnp.float32)
    weighted = (corrected * section_weight.astype(jnp.float32)).astype(jnp.bfloat16)
    tile_blocks = weighted.reshape(TILES, TH // B, B, TW // B, B).transpose(0, 1, 3, 2, 4).reshape(TILES, TB, B, B)
    picked = tile_blocks[jnp.arange(TILES)[:, None, None], source_ids]
    is_live = jnp.arange(CAP)[None, None, :] < counts[:, :, None]
    picked = jnp.where(is_live[..., None, None], picked, jnp.zeros_like(picked))
    indicator_vector = ((dest_ids[..., None] == jnp.arange(SB)[None, None, None, :]) & is_live[..., None]).astype(jnp.float32)
    strips = jnp.einsum('tdcs,tdcxy->dsxy', indicator_vector, picked.astype(jnp.float32))
    return strips.reshape(TILES * SB, B, B).astype(jnp.bfloat16)

def window_set(strips):
    extended = jnp.concatenate([strips, jnp.zeros_like(strips[:1])], 0)
    aligned = extended[:-1]
    half_shift = jnp.concatenate([extended[:-1, :, B // 2:], extended[1:, :, :B // 2]], 2)
    return jnp.stack([aligned, half_shift], 1).reshape(-1, B, B)

def exact_table(table):
    high = table.astype(jnp.bfloat16)
    low = (table - high.astype(jnp.float32)).astype(jnp.bfloat16)
    return high.astype(jnp.float32) + low.astype(jnp.float32)

def base_tables():
    positions = jnp.arange(B, dtype=jnp.int32)
    product = positions[:, None] * positions[None, :] % B
    angle = product.astype(jnp.float32) * (2.0 * math.pi / B)
    return (jnp.cos(angle), jnp.sin(angle))

def to_half(values):
    return lax.optimization_barrier(values.astype(jnp.bfloat16)).astype(jnp.float32)

def right_mult(data, table):
    return jnp.einsum('wjk,kl->wjl', data, table, precision=lax.Precision.HIGHEST)

def left_mult(table, data):
    return jnp.einsum('jk,wkl->wjl', table, data, precision=lax.Precision.HIGHEST)

def forward(windows):
    cosine, sine_table = base_tables()
    pair_right = exact_table(jnp.concatenate([cosine, sine_table], 1))
    pair_left = exact_table(jnp.concatenate([cosine, sine_table], 0))
    right = to_half(right_mult(windows.astype(jnp.float32), pair_right))
    from_cos = left_mult(pair_left, right[:, :, :B])
    from_sin = left_mult(pair_left, right[:, :, B:])
    spec_re = from_cos[:, :B] - from_sin[:, B:]
    spec_im = -(from_cos[:, B:] + from_sin[:, :B])
    return (spec_re, spec_im)

def correlate(operands):
    current, earlier = operands
    cur_re, cur_im = forward(window_set(current))
    pre_re, pre_im = forward(window_set(earlier))
    cross_re = cur_re * pre_re + cur_im * pre_im
    cross_im = cur_im * pre_re - cur_re * pre_im
    magnitude = jnp.sqrt(cross_re * cross_re + cross_im * cross_im)
    mean_mag = lax.optimization_barrier(jnp.mean(magnitude, axis=(1, 2), keepdims=True))
    denominator = magnitude + 0.1 * mean_mag + 1e-06
    whitened = to_half(jnp.concatenate([cross_re / denominator, cross_im / denominator], 2))
    cosine, sine_table = base_tables()
    inverse_right = exact_table(jnp.concatenate([jnp.concatenate([cosine, sine_table], 1), jnp.concatenate([-sine_table, cosine], 1)], 0))
    inverse_left = exact_table(jnp.concatenate([cosine, -sine_table], 1))
    rows_both = to_half(right_mult(whitened, inverse_right))
    stacked = jnp.concatenate([rows_both[:, :, :B], rows_both[:, :, B:]], 1)
    return (left_mult(inverse_left, stacked) / B).astype(jnp.float32)

def reference(image, weight, lens_filter_taps, block_src, block_dst, valid_count, anchor):
    gathered_strip_list = lax.map(render_section, (image, weight, lens_filter_taps, block_src, block_dst, valid_count))
    earlier = jnp.concatenate([anchor[None], gathered_strip_list[:-1]], 0)
    return lax.map(correlate, (gathered_strip_list, earlier))
```

```python
import functools
import math

import jax
import jax.numpy as jnp
import numpy as np
from jax import lax
from jax.experimental import pallas as pl
from jax.experimental.pallas import tpu as pltpu
from jax.sharding import PartitionSpec as P

MESH = pl.DeviceIdType.MESH
EDGE = 16
HALO = 8
CHUNK = 32
LANES = 128


def repeat(count, step):
    if count <= 4:
        for i in range(count):
            step(i)
    else:
        pl.loop(0, count)(step)


def dft_tables(size):
    half = size // 2 + 8
    positions = np.arange(size)
    angle = (positions[:, None] * positions[None, :] % size) * (2.0 * math.pi / size)
    cosine, sine = np.cos(angle), np.sin(angle)
    inverse_right = np.block([[cosine, sine], [-sine, cosine]])
    kept = np.arange(half) <= size // 2
    twice = np.where((np.arange(half) == 0) | (np.arange(half) == size // 2), 1.0, 2.0) * kept
    upper_cos, upper_sin = cosine[:half] * kept[:, None], sine[:half] * kept[:, None]
    forward_left = np.block([[upper_cos, -upper_sin], [-upper_sin, -upper_cos]])
    inverse_left = np.zeros((size, 2 * size))
    inverse_left[:, :half] = cosine[:, :half] * twice / size
    inverse_left[:, half : 2 * half] = -sine[:, :half] * twice / size
    return jnp.asarray(np.concatenate([inverse_right, forward_left, inverse_left], 0), jnp.bfloat16)


def lens(rows, taps, first, count):
    left, middle, right = rows
    lane = lax.broadcasted_iota(jnp.int32, middle.shape, 1)
    shifted = []
    for off in range(-2, 3):
        if off == 0:
            shifted.append(middle)
        elif off > 0:
            mixed = jnp.where(lane < off, right, middle)
            shifted.append(pltpu.roll(mixed, LANES - off, 1))
        else:
            mixed = jnp.where(lane >= LANES + off, left, middle)
            shifted.append(pltpu.roll(mixed, -off, 1))
    total = None
    n = middle.shape[0]
    for a in range(5):
        part = taps[5 * a] * shifted[0]
        for b in range(1, 5):
            part = part + taps[5 * a + b] * shifted[b]
        if a != 2:
            part = pltpu.roll(part, (2 - a) % n, 0)
        part = part[first : first + count]
        total = part if total is None else total + part
    return total


def shifts(left, middle, right):
    lane = lax.broadcasted_iota(jnp.int32, middle.shape, 1)
    shifted = []
    for off in range(-2, 3):
        if off == 0:
            shifted.append(middle)
        elif off > 0:
            shifted.append(pltpu.roll(jnp.where(lane < off, right, middle), LANES - off, 1))
        else:
            shifted.append(pltpu.roll(jnp.where(lane >= LANES + off, left, middle), -off, 1))
    return shifted


def kernel(
    sections,
    tiles,
    image,
    weight,
    anchor,
    tables,
    taps_any,
    src_any,
    dst_any,
    valid_any,
    out,
    taps_ref,
    src_ref,
    dst_ref,
    valid_ref,
    img,
    wgt,
    halo,
    cor,
    out_buf,
    in_buf,
    out_cor,
    in_cor,
    strip,
    pre,
    strip_cor,
    pre_cor,
    rim_out,
    rim_own,
    rim_pre,
    spec,
    tab,
    load_sem,
    halo_send,
    halo_recv,
    block_send,
    block_recv,
    cor_send,
    cor_recv,
    strip_send,
    strip_recv,
    rim_send,
    rim_recv,
    next_send,
    next_recv,
):
    sec = lax.axis_index("sec")
    me = lax.axis_index("tile")
    th, tw = image.shape[1:]
    side = wgt.shape[1]
    chunks, blocks = strip.shape[0], strip.shape[1] - 1
    cap = in_buf.shape[2]
    across, down = tw // side, th // side
    padded = across + 2
    half = side // 2 + 8
    pairs = chunks // 2

    barrier = pltpu.get_barrier_semaphore()

    def greet(target):
        pl.semaphore_signal(barrier, inc=1, device_id=target, device_id_type=MESH)

    for k in range(1, tiles):
        greet((sec, lax.rem(me + k, tiles)))
    has_next, has_prev = sec < sections - 1, sec > 0
    not_first, not_last = me > 0, me < tiles - 1

    @pl.when(has_next)
    def _():
        greet((sec + 1, me))

    @pl.when(has_next & not_first)
    def _():
        greet((sec + 1, me - 1))

    @pl.when(has_prev)
    def _():
        greet((sec - 1, me))

    @pl.when(has_prev & not_last)
    def _():
        greet((sec - 1, me + 1))

    loads = []
    for source, ref in (
        (taps_any, taps_ref),
        (src_any, src_ref),
        (dst_any, dst_ref),
        (valid_any, valid_ref),
    ):
        loads.append(pltpu.make_async_copy(source, ref, load_sem.at[len(loads)]))
    for r in range(down):
        low, high = max(0, r * side - EDGE), min(th, (r + 1) * side + EDGE)
        place = low - (r * side - EDGE)
        for c in range(across):
            columns = pl.ds(c * side, side)
            loads.append(
                pltpu.make_async_copy(
                    image.at[0, pl.ds(low, high - low), columns],
                    img.at[r * padded + c + 1, pl.ds(place, high - low)],
                    load_sem.at[len(loads)],
                )
            )
            loads.append(
                pltpu.make_async_copy(
                    weight.at[0, pl.ds(r * side, side), columns],
                    wgt.at[r * across + c],
                    load_sem.at[len(loads)],
                )
            )
    table_load = pltpu.make_async_copy(tables, tab, load_sem.at[len(loads)])
    for load in loads:
        load.start()
    table_load.start()

    def strip_at(c, j):
        return c if c < chunks - 1 else chunks - 1 + j

    def anchor_copy(c, j, count):
        return pltpu.make_async_copy(
            anchor.at[pl.ds(j, count), pl.ds(c * CHUNK, CHUNK)],
            pre.at[c, pl.ds(j, count)],
            strip_recv.at[strip_at(c, j)],
        )

    @pl.when(sec == 0)
    def _():
        for c in range(chunks - 1):
            anchor_copy(c, 0, blocks).start()
        repeat(blocks, lambda j: anchor_copy(chunks - 1, j, 1).start())
        pre_cor[...] = jnp.zeros(pre_cor.shape, pre_cor.dtype)

    zeros = jnp.zeros(img.shape[1:], img.dtype)
    for r in range(down):
        img[r * padded] = zeros
        img[(r + 1) * padded - 1] = zeros
    for c in range(across):
        img[c + 1, :EDGE] = zeros[:EDGE]
        img[(down - 1) * padded + c + 1, EDGE + side :] = zeros[:EDGE]

    @pl.when(me == 0)
    def _():
        halo[0] = jnp.zeros(halo.shape[1:], halo.dtype)

    @pl.when(me == tiles - 1)
    def _():
        halo[1] = jnp.zeros(halo.shape[1:], halo.dtype)
        for c in range(chunks):
            for ref in (strip, pre):
                ref[c, blocks] = jnp.zeros(ref.shape[2:], ref.dtype)
        for ref in (strip_cor, pre_cor):
            ref[blocks] = jnp.zeros(ref.shape[1:], ref.dtype)

    def remote(src, dst, send, recv, target):
        return pltpu.make_async_remote_copy(
            src_ref=src,
            dst_ref=dst,
            send_sem=send,
            recv_sem=recv,
            device_id=target,
            device_id_type=MESH,
        )

    after_me, before_me = lax.rem(me + 1, tiles), lax.rem(me + tiles - 1, tiles)
    next_sec = lax.rem(sec + 1, sections)
    halo_down = remote(
        image.at[0, pl.ds(th - HALO, HALO)],
        halo.at[0],
        halo_send.at[0],
        halo_recv.at[0],
        (sec, after_me),
    )
    halo_up = remote(
        image.at[0, pl.ds(0, HALO)],
        halo.at[1],
        halo_send.at[1],
        halo_recv.at[1],
        (sec, before_me),
    )

    def onward(c):
        here = pl.ds(0, blocks)
        return remote(
            strip.at[c, here], pre.at[c, here], strip_send.at[c], strip_recv.at[c], (next_sec, me)
        )

    def onward_last(j):
        at = chunks - 1 + j
        return remote(
            strip.at[chunks - 1, j],
            pre.at[chunks - 1, j],
            strip_send.at[at],
            strip_recv.at[at],
            (next_sec, me),
        )

    def own_rim(p):
        return remote(rim_out.at[p], rim_own.at[p], rim_send.at[p], rim_recv.at[p], (sec, before_me))

    def onward_rim(p):
        return remote(
            rim_out.at[p], rim_pre.at[p], next_send.at[p], next_recv.at[p], (next_sec, before_me)
        )

    def anchor_rim(p):
        return remote(
            rim_out.at[pairs + p],
            rim_pre.at[p],
            next_send.at[pairs + 2 + p],
            next_recv.at[p],
            (sec, before_me),
        )

    own_rim_cor = remote(
        strip_cor.at[0], strip_cor.at[blocks], rim_send.at[pairs], rim_recv.at[pairs], (sec, before_me)
    )
    onward_rim_cor = remote(
        strip_cor.at[0],
        pre_cor.at[blocks],
        next_send.at[pairs],
        next_recv.at[pairs],
        (next_sec, before_me),
    )
    onward_cor = remote(
        strip_cor.at[pl.ds(0, blocks)],
        pre_cor.at[pl.ds(0, blocks)],
        next_send.at[pairs + 1],
        next_recv.at[pairs + 1],
        (next_sec, me),
    )

    for load in loads:
        load.wait()

    taps = [taps_ref[0, 0, k] for k in range(25)]
    chips = tiles // 2

    def owner(k):
        chip = lax.rem(me // 2 + 1 + k // 2, chips)
        return chip * 2 + lax.rem(me + 1 + k, 2)

    def live(target, slot):
        return jnp.clip(valid_ref[0, 0, target] - slot, 0, 1).astype(jnp.float32)

    def fill(k, c, ref, place):
        target = owner(k)
        first = pl.multiple_of(c * CHUNK, CHUNK)
        for slot in range(cap):
            source = src_ref[0, 0, slot, target]
            at = source + 2 * lax.div(source, across)
            rows = [
                img[at + n, pl.ds(first, CHUNK + 2 * EDGE)].astype(jnp.float32) for n in range(3)
            ]
            rows = [part[EDGE - 8 : EDGE + CHUNK + 8] for part in rows]
            corrected = lens(rows, taps, 8, CHUNK)
            factor = wgt[source, pl.ds(first, CHUNK)].astype(jnp.float32)
            ref[place, c, slot] = (corrected * factor * live(target, slot)).astype(jnp.bfloat16)

    def block_copy(k, c):
        target = owner(k)
        return remote(
            out_buf.at[target, c],
            in_buf.at[me, c],
            block_send.at[target, c],
            block_recv.at[me, c],
            (sec, target),
        )

    def block_from(k, c):
        source = owner(k)
        return remote(
            out_buf.at[source, c],
            in_buf.at[source, c],
            block_send.at[source, c],
            block_recv.at[source, c],
            (sec, source),
        )

    def cor_copy(k):
        target = owner(k)
        return remote(
            out_cor.at[target], in_cor.at[me], cor_send.at[target], cor_recv.at[me], (sec, target)
        )

    def cor_from(k):
        source = owner(k)
        return remote(
            out_cor.at[source], in_cor.at[source], cor_send.at[source], cor_recv.at[source], (sec, source)
        )

    def pack_rim(ref, p, place):
        low, high = ref[2 * p, 0].astype(jnp.float32), ref[2 * p + 1, 0].astype(jnp.float32)
        lane = lax.broadcasted_iota(jnp.int32, low.shape, 1)
        rim_out[place] = jnp.where(lane < side // 2, low, pltpu.roll(high, side // 2, 1)).astype(
            rim_out.dtype
        )

    def unpack_rim(rim, ref):
        for p in range(pairs):
            packed = rim[p]
            ref[2 * p, blocks] = packed
            ref[2 * p + 1, blocks] = pltpu.roll(packed.astype(jnp.float32), side // 2, 1).astype(
                packed.dtype
            )

    fill(0, 0, out_buf, owner(0))
    after, before = has_next.astype(jnp.int32), has_prev.astype(jnp.int32)
    peers = after * (1 + not_first.astype(jnp.int32)) + before * (1 + not_last.astype(jnp.int32))
    pl.semaphore_wait(barrier, tiles - 1 + peers)

    @pl.when(not_last)
    def _():
        halo_down.start()

    @pl.when(not_first)
    def _():
        halo_up.start()

    block_copy(0, 0).start()

    def send_of(c):
        def step(k):
            fill(k, c, out_buf, owner(k))
            block_copy(k, c).start()

        return step

    pl.loop(1, tiles - 1)(send_of(0))
    fill(tiles - 1, 0, in_buf, me)

    def send_chunk(c):
        pl.loop(0, tiles - 1)(send_of(c))
        fill(tiles - 1, c, in_buf, me)

    pl.loop(1, chunks)(send_chunk)

    @pl.when(not_first)
    def _():
        halo_down.wait_recv()

    @pl.when(not_last)
    def _():
        halo_up.wait_recv()

    row = lax.broadcasted_iota(jnp.int32, (HALO, LANES), 0)

    def halo_terms(n, steps):
        none = jnp.zeros((HALO, LANES), jnp.float32)
        columns = [
            halo[n, :, c * side : (c + 1) * side].astype(jnp.float32) for c in range(across)
        ]
        for c in range(across):
            left = columns[c - 1] if c > 0 else none
            right = columns[c + 1] if c < across - 1 else none
            moved = shifts(left, columns[c], right)
            total = none
            for a, step, kept in steps:
                part = taps[5 * a] * moved[0]
                for b in range(1, 5):
                    part = part + taps[5 * a + b] * moved[b]
                total = total + jnp.where(kept, pltpu.roll(part, step, 0), 0.0)
            yield c, total

    if down > 2:
        for at in range(across, (down - 1) * across):
            cor[at] = jnp.zeros(cor.shape[1:], cor.dtype)
    for c, total in halo_terms(0, ((0, 2, row < 2), (1, 1, row < 1))):
        cor[c] = total * wgt[c, :EDGE].astype(jnp.float32)[:HALO]
    for c, total in halo_terms(1, ((4, 6, row >= 6), (3, 7, row >= 7))):
        at = (down - 1) * across + c
        total = total * wgt[at, side - EDGE :].astype(jnp.float32)[EDGE - HALO :]
        cor[at] = total if down > 1 else cor[at] + total

    def fill_cor(k, ref, place):
        target = owner(k)
        terms = [cor[src_ref[0, 0, slot, target]] * live(target, slot) for slot in range(cap)]
        ref[place] = jnp.concatenate(terms, 0).astype(jnp.bfloat16)

    def send_cor(k):
        fill_cor(k, out_cor, owner(k))
        cor_copy(k).start()

    pl.loop(0, tiles - 1)(send_cor)
    fill_cor(tiles - 1, in_cor, me)

    @pl.when((sec == 0) & not_first)
    def _():
        for c in range(chunks - 1):
            anchor_copy(c, 0, blocks).wait()
        anchor_copy(chunks - 1, 0, 1).wait()
        for p in range(pairs):
            pack_rim(pre, p, pairs + p)
            anchor_rim(p).start()

    def summed(part):
        totals = [None] * blocks
        for t in range(tiles):
            for slot in range(cap):
                value = part(t, slot).astype(jnp.float32)
                place = dst_ref[0, 0, slot, t]
                for j in range(blocks):
                    term = value * (1 - jnp.minimum(jnp.abs(place - j), 1)).astype(jnp.float32)
                    totals[j] = term if totals[j] is None else totals[j] + term
        return [total.astype(jnp.bfloat16) for total in totals]

    def gather_chunk(c):
        repeat(tiles - 1, lambda k: block_from(k, c).wait_recv())
        for j, value in enumerate(summed(lambda t, slot: in_buf[t, c, slot])):
            strip[c, j] = value

    def start_rim(p):
        pack_rim(strip, p, p)

        @pl.when(has_next & not_first)
        def _():
            onward_rim(p).start()

        @pl.when(not_first)
        def _():
            own_rim(p).start()

    for c in range(chunks - 1):
        gather_chunk(c)

        @pl.when(has_next)
        def _():
            onward(c).start()

        if c % 2 == 1:
            start_rim(c // 2)

    repeat(tiles - 1, lambda k: cor_from(k).wait_recv())
    cors = [in_cor[t].astype(jnp.float32) for t in range(tiles)]
    for j, value in enumerate(summed(lambda t, slot: cors[t][slot * HALO : (slot + 1) * HALO])):
        strip_cor[j] = value

    @pl.when(has_next & not_first)
    def _():
        onward_rim_cor.start()

    @pl.when(has_next)
    def _():
        onward_cor.start()

    @pl.when(not_first)
    def _():
        own_rim_cor.start()

    gather_chunk(chunks - 1)
    start_rim(pairs - 1)

    @pl.when(has_next)
    def _():
        repeat(blocks, lambda k: onward_last(blocks - 1 - k).start())

    table_load.wait()
    right_table = tab.at[pl.ds(0, 2 * side)]
    left_table = tab.at[pl.ds(2 * side, 2 * half)]
    inverse_table = tab.at[pl.ds(2 * side + 2 * half, side)]

    def whole(ref, cor_ref, m):
        fix = cor_ref[m].astype(jnp.float32)
        rows = lax.broadcasted_iota(jnp.int32, fix.shape, 0)
        none = jnp.zeros_like(fix)
        top = jnp.concatenate([jnp.where(rows < HALO // 2, fix, 0.0), none], 0)
        bottom = jnp.concatenate([none, jnp.where(rows >= HALO // 2, fix, 0.0)], 0)
        parts = [ref[c, m] for c in range(chunks)]
        first, last = parts[0], parts[-1]
        parts[0] = jnp.concatenate(
            [(first[:16].astype(jnp.float32) + top).astype(first.dtype), first[16:]], 0
        )
        parts[-1] = jnp.concatenate(
            [last[: CHUNK - 16], (last[CHUNK - 16 :].astype(jnp.float32) + bottom).astype(last.dtype)], 0
        )
        return jnp.concatenate(parts, 0)

    def spectra(ref, cor_ref, m):
        block, after = whole(ref, cor_ref, m), whole(ref, cor_ref, m + 1)
        lane = lax.broadcasted_iota(jnp.int32, block.shape, 1)
        shifted = jnp.where(
            lane < side // 2, after.astype(jnp.float32), block.astype(jnp.float32)
        ).astype(block.dtype)
        windows = jnp.concatenate([block, shifted], 0)
        right = jnp.dot(
            windows, right_table[:side], preferred_element_type=jnp.float32
        ).astype(jnp.bfloat16)
        stacked = jnp.concatenate(
            [
                jnp.concatenate([right[:side, :side], right[:side, side:]], 0),
                jnp.concatenate([right[side:, :side], right[side:, side:]], 0),
            ],
            1,
        )
        return jnp.dot(left_table[...], stacked, preferred_element_type=jnp.float32)

    def keep(m):
        spec[m] = spectra(strip, strip_cor, m)

    repeat(blocks - 1, keep)

    @pl.when(not_last)
    def _():
        for p in range(pairs):
            own_rim(p).wait_recv()
        own_rim_cor.wait_recv()
        unpack_rim(rim_own, strip)

    keep(blocks - 1)

    for c in range(chunks - 1):

        @pl.when(has_prev | (me == 0))
        def _():
            onward(c).wait_recv()

    @pl.when(has_prev)
    def _():
        onward_cor.wait_recv()

    @pl.when(has_prev & not_last)
    def _():
        onward_rim_cor.wait_recv()

    @pl.when(not_last)
    def _():
        for p in range(pairs):
            onward_rim(p).wait_recv()
        unpack_rim(rim_pre, pre)

    def correlate(k):
        m = blocks - 1 - k

        @pl.when(has_prev | (me == 0) | (m > 0))
        def _():
            onward_last(m).wait_recv()

        earlier = spectra(pre, pre_cor, m)
        current = spec[m]
        cur_re, cur_im = current[:half], current[half:]
        pre_re, pre_im = earlier[:half], earlier[half:]
        cross_re = cur_re * pre_re + cur_im * pre_im
        cross_im = cur_im * pre_re - cur_re * pre_im
        magnitude = jnp.sqrt(cross_re * cross_re + cross_im * cross_im)
        rows = lax.broadcasted_iota(jnp.int32, (8, side), 0)
        ends = jnp.where(rows < 1, 1.0, 2.0)
        whitened = []
        for n in range(2):
            cols = slice(n * side, (n + 1) * side)
            mag = magnitude[:, cols]
            inner = mag[8:16]
            for at in range(16, half - 8, 8):
                inner = inner + mag[at : at + 8]
            total = 2.0 * inner + ends * (mag[:8] + mag[half - 8 :])
            mean = jnp.sum(total) * (1.0 / (side * side))
            scale = 1.0 / (mag + (0.1 * mean + 1e-06))
            whitened.append(
                jnp.concatenate([cross_re[:, cols] * scale, cross_im[:, cols] * scale], 1)
            )
        whitened = jnp.concatenate(whitened, 0).astype(jnp.bfloat16)
        rows_both = jnp.dot(whitened, right_table[...], preferred_element_type=jnp.float32)
        stacked = jnp.concatenate(
            [
                jnp.concatenate([rows_both[:half, :side], rows_both[:half, side:]], 0),
                jnp.concatenate([rows_both[half:, :side], rows_both[half:, side:]], 0),
            ],
            1,
        ).astype(jnp.bfloat16)
        result = jnp.dot(
            inverse_table[...][:, : 2 * half], stacked, preferred_element_type=jnp.float32
        )
        out[0, 2 * m] = result[:, :side]
        out[0, 2 * m + 1] = result[:, side:]

    repeat(blocks, correlate)

    @pl.when(not_last)
    def _():
        halo_down.wait_send()

    @pl.when(not_first)
    def _():
        halo_up.wait_send()
        for p in range(pairs):
            own_rim(p).wait_send()
        own_rim_cor.wait_send()

    @pl.when(has_next)
    def _():
        for c in range(chunks - 1):
            onward(c).wait_send()
        repeat(blocks, lambda j: onward_last(j).wait_send())
        onward_cor.wait_send()

    @pl.when((sec == 0) & not_first)
    def _():
        for p in range(pairs):
            anchor_rim(p).wait_send()

    @pl.when(has_next & not_first)
    def _():
        for p in range(pairs):
            onward_rim(p).wait_send()
        onward_rim_cor.wait_send()

    def left_here(k):
        for c in range(chunks):
            block_copy(k, c).wait_send()
        cor_copy(k).wait_send()

    repeat(tiles - 1, left_here)


def solution(mesh):
    sections, tiles = mesh.shape["sec"], mesh.shape["tile"]

    def body(image, weight, lens_filter_taps, block_src, block_dst, valid_count, anchor):
        th, tw = image.shape[1:]
        blocks, side = anchor.shape[:2]
        cap = block_src.shape[-1]
        anywhere = pl.BlockSpec(memory_space=pl.ANY)
        bf16 = jnp.bfloat16
        dma = pltpu.SemaphoreType.DMA
        across, down = tw // side, th // side
        chunks, half = side // CHUNK, side // 2 + 8
        pairs = chunks // 2
        tables = dft_tables(side)
        return pl.pallas_call(
            functools.partial(kernel, sections, tiles),
            out_shape=pltpu.VMEM((1, 2 * blocks, side, side), jnp.float32),
            in_specs=[anywhere] * 8,
            out_specs=pl.BlockSpec(memory_space=pltpu.VMEM),
            scratch_shapes=[
                pltpu.SMEM(lens_filter_taps.shape, jnp.float32),
                pltpu.SMEM((1, 1, cap, tiles), jnp.int32),
                pltpu.SMEM((1, 1, cap, tiles), jnp.int32),
                pltpu.SMEM(valid_count.shape, jnp.int32),
                pltpu.VMEM((down * (across + 2), side + 2 * EDGE, side), bf16),
                pltpu.VMEM((down * across, side, side), bf16),
                pltpu.VMEM((2, HALO, tw), bf16),
                pltpu.VMEM((down * across, HALO, side), jnp.float32),
                pltpu.VMEM((tiles, chunks, cap, CHUNK, side), bf16),
                pltpu.VMEM((tiles, chunks, cap, CHUNK, side), bf16),
                pltpu.VMEM((tiles, cap * HALO, side), bf16),
                pltpu.VMEM((tiles, cap * HALO, side), bf16),
                pltpu.VMEM((chunks, blocks + 1, CHUNK, side), bf16),
                pltpu.VMEM((chunks, blocks + 1, CHUNK, side), bf16),
                pltpu.VMEM((blocks + 1, HALO, side), bf16),
                pltpu.VMEM((blocks + 1, HALO, side), bf16),
                pltpu.VMEM((2 * pairs, CHUNK, side), bf16),
                pltpu.VMEM((pairs, CHUNK, side), bf16),
                pltpu.VMEM((pairs, CHUNK, side), bf16),
                pltpu.VMEM((blocks, 2 * half, 2 * side), jnp.float32),
                pltpu.VMEM(tables.shape, bf16),
                dma((2 * down * across + 5,)),
                dma((2,)),
                dma((2,)),
                dma((tiles, chunks)),
                dma((tiles, chunks)),
                dma((tiles,)),
                dma((tiles,)),
                dma((chunks - 1 + blocks,)),
                dma((chunks - 1 + blocks,)),
                dma((pairs + 1,)),
                dma((pairs + 1,)),
                dma((2 * pairs + 2,)),
                dma((pairs + 2,)),
            ],
            compiler_params=pltpu.CompilerParams(collective_id=0, has_side_effects=True),
        )(
            image,
            weight,
            anchor,
            tables,
            lens_filter_taps,
            block_src.transpose(0, 1, 3, 2),
            block_dst.transpose(0, 2, 3, 1),
            valid_count,
        )

    in_specs = (
        P("sec", "tile", None),
        P("sec", "tile", None),
        P("sec", "tile", None),
        P("sec", "tile", None, None),
        P("sec", None, "tile", None),
        P("sec", "tile", None),
        P("tile", None, None),
    )
    out_specs = P("sec", "tile", None, None)
    return jax.shard_map(body, mesh=mesh, in_specs=in_specs, out_specs=out_specs, check_vma=False)
```

```python
import functools
import math

import jax
import jax.numpy as jnp
import numpy as np
from jax import lax
from jax.experimental import pallas as pl
from jax.experimental.pallas import tpu as pltpu
from jax.sharding import PartitionSpec as P

MESH = pl.DeviceIdType.MESH
EDGE = 8
HALO = 8
CHUNK = 32
LANES = 128


def repeat(count, step):
    if count <= 4:
        for i in range(count):
            step(i)
    else:
        pl.loop(0, count)(step)


def dft_tables(size):
    half = size // 2 + 8
    positions = np.arange(size)
    angle = (positions[:, None] * positions[None, :] % size) * (2.0 * math.pi / size)
    cosine, sine = np.cos(angle), np.sin(angle)
    inverse_right = np.block([[cosine, sine], [-sine, cosine]])
    kept = np.arange(half) <= size // 2
    twice = np.where((np.arange(half) == 0) | (np.arange(half) == size // 2), 1.0, 2.0) * kept
    upper_cos, upper_sin = cosine[:half] * kept[:, None], sine[:half] * kept[:, None]
    forward_left = np.zeros((2 * half, 2 * size))
    forward_left[:, :size] = np.concatenate([upper_cos, upper_sin], 0)
    inverse_left = np.zeros((size, 2 * size))
    inverse_left[:, :half] = cosine[:, :half] * twice / size
    inverse_left[:, half : 2 * half] = -sine[:, :half] * twice / size
    return jnp.asarray(np.concatenate([inverse_right, forward_left, inverse_left], 0), jnp.bfloat16)


def lens(rows, taps, first, count):
    left, middle, right = rows
    lane = lax.broadcasted_iota(jnp.int32, middle.shape, 1)
    shifted = []
    for off in range(-2, 3):
        if off == 0:
            shifted.append(middle)
        elif off > 0:
            mixed = jnp.where(lane < off, right, middle)
            shifted.append(pltpu.roll(mixed, LANES - off, 1))
        else:
            mixed = jnp.where(lane >= LANES + off, left, middle)
            shifted.append(pltpu.roll(mixed, -off, 1))
    total = None
    n = middle.shape[0]
    for a in range(5):
        part = taps[5 * a] * shifted[0]
        for b in range(1, 5):
            part = part + taps[5 * a + b] * shifted[b]
        if a != 2:
            part = pltpu.roll(part, (2 - a) % n, 0)
        part = part[first : first + count]
        total = part if total is None else total + part
    return total


def shifts(left, middle, right):
    lane = lax.broadcasted_iota(jnp.int32, middle.shape, 1)
    shifted = []
    for off in range(-2, 3):
        if off == 0:
            shifted.append(middle)
        elif off > 0:
            shifted.append(pltpu.roll(jnp.where(lane < off, right, middle), LANES - off, 1))
        else:
            shifted.append(pltpu.roll(jnp.where(lane >= LANES + off, left, middle), -off, 1))
    return shifted


def kernel(
    sections,
    tiles,
    image,
    weight,
    anchor,
    tables,
    taps_any,
    src_any,
    dst_any,
    valid_any,
    out,
    taps_ref,
    src_ref,
    dst_ref,
    valid_ref,
    img,
    img_late,
    wgt,
    wgt_late,
    halo,
    cor,
    out_buf,
    in_buf,
    out_cor,
    in_cor,
    strip,
    pre,
    strip_cor,
    pre_cor,
    rim_out,
    rim_anchor,
    rim_own,
    rim_pre,
    spread,
    spec,
    tab,
    places,
    load_sem,
    halo_send,
    halo_recv,
    block_recv,
    strip_recv,
    send_sem,
    recv_sem,
):
    sec = lax.axis_index("sec")
    me = lax.axis_index("tile")
    th, tw = image.shape[1:]
    side = anchor.shape[1]
    chunks, blocks = strip.shape[0], strip.shape[1] - 1
    cap = in_buf.shape[2]
    groups = blocks // 2
    block_send, cor_send, strip_send, strip_cor_send, own_send, next_send, anchor_send = (
        send_sem.at[n] for n in range(7)
    )
    cor_recv, strip_cor_recv, own_recv, next_recv = (recv_sem.at[n] for n in range(4))
    across, down = tw // side, th // side
    padded = across + 2
    half = side // 2 + 8
    pairs = chunks // 2

    barrier = pltpu.get_barrier_semaphore()

    def greet(target):
        pl.semaphore_signal(barrier, inc=1, device_id=target, device_id_type=MESH)

    for k in range(1, tiles):
        greet((sec, lax.rem(me + k, tiles)))
    has_next, has_prev = sec < sections - 1, sec > 0
    not_first, not_last = me > 0, me < tiles - 1

    @pl.when(has_next)
    def _():
        greet((sec + 1, me))

    @pl.when(has_next & not_first)
    def _():
        greet((sec + 1, me - 1))

    @pl.when(has_prev)
    def _():
        greet((sec - 1, me))

    @pl.when(has_prev & not_last)
    def _():
        greet((sec - 1, me + 1))

    loads = []
    for source, ref in (
        (taps_any, taps_ref),
        (src_any, src_ref),
        (dst_any, dst_ref),
        (valid_any, valid_ref),
    ):
        loads.append(pltpu.make_async_copy(source, ref, load_sem.at[len(loads)]))
    early, late = [], []
    early_rows = late_rows = 0
    for r in range(down):
        start, end = r * side - EDGE, (r + 1) * side + EDGE
        top, split = max(0, start), r * side + CHUNK + EDGE
        again, bottom = split - 2 * EDGE, min(th, end)
        early_rows, late_rows = early_rows + split - top, late_rows + bottom - again
        for c in range(across):
            columns = pl.ds(c * side, side)
            at, n = r * padded + c + 1, r * across + c
            early.append(
                pltpu.make_async_copy(
                    image.at[0, pl.ds(top, split - top), columns],
                    img.at[at, pl.ds(top - start, split - top)],
                    load_sem.at[4],
                )
            )
            early.append(
                pltpu.make_async_copy(
                    weight.at[0, pl.ds(r * side, CHUNK), columns], wgt.at[n], load_sem.at[5]
                )
            )
            late.append(
                pltpu.make_async_copy(
                    image.at[0, pl.ds(again, bottom - again), columns],
                    img_late.at[at, pl.ds(0, bottom - again)],
                    load_sem.at[6],
                )
            )
            late.append(
                pltpu.make_async_copy(
                    weight.at[0, pl.ds(r * side + CHUNK, side - CHUNK), columns],
                    wgt_late.at[n],
                    load_sem.at[7],
                )
            )

    def landed(ref, sem):
        pltpu.make_async_copy(ref, ref, sem).wait()

    every = pl.ds(0, down * across)
    table_load = pltpu.make_async_copy(tables, tab, load_sem.at[8])
    for load in loads + early + late:
        load.start()
    table_load.start()

    low_chunks, low_blocks = pl.ds(0, chunks - 1), pl.ds(0, blocks)

    def anchor_copy(c):
        return pltpu.make_async_copy(
            anchor.at[:, pl.ds(c * CHUNK, CHUNK)], pre.at[c, low_blocks], strip_recv.at[0]
        )

    def anchor_last(g):
        return pltpu.make_async_copy(
            anchor.at[pl.ds(2 * g, 2), pl.ds((chunks - 1) * CHUNK, CHUNK)],
            pre.at[chunks - 1, pl.ds(2 * g, 2)],
            strip_recv.at[1 + g],
        )

    @pl.when(sec == 0)
    def _():
        for c in range(chunks - 1):
            anchor_copy(c).start()
        repeat(groups, lambda g: anchor_last(g).start())
        pre_cor[...] = jnp.zeros(pre_cor.shape, pre_cor.dtype)

    for ref in (img, img_late):
        zeros = jnp.zeros(ref.shape[1:], ref.dtype)
        for r in range(down):
            ref[r * padded] = zeros
            ref[(r + 1) * padded - 1] = zeros
    for c in range(across):
        img[c + 1, :EDGE] = zeros[:EDGE]
        img_late[(down - 1) * padded + c + 1, -EDGE:] = zeros[:EDGE]

    @pl.when(me == 0)
    def _():
        halo[0] = jnp.zeros(halo.shape[1:], halo.dtype)

    @pl.when(me == tiles - 1)
    def _():
        halo[1] = jnp.zeros(halo.shape[1:], halo.dtype)
        for c in range(chunks):
            for ref in (strip, pre):
                ref[c, blocks] = jnp.zeros(ref.shape[2:], ref.dtype)

    def remote(src, dst, send, recv, target):
        return pltpu.make_async_remote_copy(
            src_ref=src,
            dst_ref=dst,
            send_sem=send,
            recv_sem=recv,
            device_id=target,
            device_id_type=MESH,
        )

    after_me, before_me = lax.rem(me + 1, tiles), lax.rem(me + tiles - 1, tiles)
    next_sec = lax.rem(sec + 1, sections)
    halo_down = remote(
        image.at[0, pl.ds(th - HALO, HALO)],
        halo.at[0],
        halo_send.at[0],
        halo_recv.at[0],
        (sec, after_me),
    )
    halo_up = remote(
        image.at[0, pl.ds(0, HALO)],
        halo.at[1],
        halo_send.at[1],
        halo_recv.at[1],
        (sec, before_me),
    )

    rim_rows = pairs * CHUNK

    def onward(c):
        return remote(
            strip.at[c, low_blocks],
            pre.at[c, low_blocks],
            strip_send,
            strip_recv.at[0],
            (next_sec, me),
        )

    def onward_last(g):
        here = pl.ds(2 * g, 2)
        return remote(
            strip.at[chunks - 1, here],
            pre.at[chunks - 1, here],
            strip_send,
            strip_recv.at[1 + g],
            (next_sec, me),
        )

    onward_cor = remote(strip_cor, pre_cor, strip_cor_send, strip_cor_recv, (next_sec, me))
    anchor_rim = remote(rim_anchor, rim_pre, anchor_send, next_recv, (sec, before_me))

    def rim_copies(first, count):
        rows = pl.ds(first, count)
        return (
            remote(rim_out.at[rows], rim_own.at[rows], own_send, own_recv, (sec, before_me)),
            remote(rim_out.at[rows], rim_pre.at[rows], next_send, next_recv, (next_sec, before_me)),
        )

    for load in loads:
        load.wait()
    landed(img.at[every, pl.ds(0, early_rows // down)], load_sem.at[4])
    landed(wgt, load_sem.at[5])

    taps = [taps_ref[0, 0, k] for k in range(25)]
    chips = tiles // 2

    def owner(k):
        chip = lax.rem(me // 2 + 1 + k // 2, chips)
        return chip * 2 + lax.rem(me + 1 + k, 2)

    def live(target, slot):
        return jnp.clip(valid_ref[0, 0, target] - slot, 0, 1).astype(jnp.float32)

    def fill(k, c, ref, place, pixels, factors):
        target = owner(k)
        first = 0 if pixels is img else pl.multiple_of((c - 1) * CHUNK, CHUNK)
        for slot in range(cap):
            source = src_ref[0, 0, slot, target]
            at = source + 2 * lax.div(source, across)
            rows = [
                pixels[at + n, pl.ds(first, CHUNK + 2 * EDGE)].astype(jnp.float32) for n in range(3)
            ]
            corrected = lens(rows, taps, EDGE, CHUNK)
            factor = factors[source, pl.ds(first, CHUNK)].astype(jnp.float32)
            ref[c, place, slot] = (corrected * factor * live(target, slot)).astype(jnp.bfloat16)

    def block_copy(k, c):
        target = owner(k)
        return remote(
            out_buf.at[c, target], in_buf.at[c, me], block_send, block_recv.at[c], (sec, target)
        )

    def cor_copy(k):
        target = owner(k)
        return remote(out_cor.at[target], in_cor.at[me], cor_send, cor_recv, (sec, target))

    others = pl.ds(0, tiles - 1)

    def packed_rim(ref, p):
        low, high = ref[2 * p, 0].astype(jnp.float32), ref[2 * p + 1, 0].astype(jnp.float32)
        lane = lax.broadcasted_iota(jnp.int32, low.shape, 1)
        return jnp.where(lane < side // 2, low, pltpu.roll(high, side // 2, 1)).astype(ref.dtype)

    def mended(first, last, fix):
        rows = lax.broadcasted_iota(jnp.int32, fix.shape, 0)
        none = jnp.zeros_like(fix)
        top = jnp.concatenate([jnp.where(rows < HALO // 2, fix, 0.0), none], 0)
        bottom = jnp.concatenate([none, jnp.where(rows >= HALO // 2, fix, 0.0)], 0)
        kind = first.dtype
        first = jnp.concatenate([(first[:16].astype(jnp.float32) + top).astype(kind), first[16:]], 0)
        last = jnp.concatenate(
            [last[: CHUNK - 16], (last[CHUNK - 16 :].astype(jnp.float32) + bottom).astype(kind)], 0
        )
        return first, last

    def unpack_rim(rim, ref):
        parts = []
        for p in range(pairs):
            packed = rim[p * CHUNK : (p + 1) * CHUNK]
            turned = pltpu.roll(packed.astype(jnp.float32), side // 2, 1).astype(packed.dtype)
            parts += [packed, turned]
        fix = rim[rim_rows:].astype(jnp.float32)
        parts[0], parts[-1] = mended(parts[0], parts[-1], fix)
        for c in range(chunks):
            ref[c, blocks] = parts[c]

    fill(0, 0, out_buf, owner(0), img, wgt)
    after, before = has_next.astype(jnp.int32), has_prev.astype(jnp.int32)
    peers = after * (1 + not_first.astype(jnp.int32)) + before * (1 + not_last.astype(jnp.int32))
    pl.semaphore_wait(barrier, tiles - 1 + peers)

    @pl.when(not_last)
    def _():
        halo_down.start()

    @pl.when(not_first)
    def _():
        halo_up.start()

    block_copy(0, 0).start()

    def send_of(c, *held):
        def step(k):
            fill(k, c, out_buf, owner(k), *held)
            block_copy(k, c).start()

        return step

    pl.loop(1, tiles - 1)(send_of(0, img, wgt))
    fill(tiles - 1, 0, in_buf, me, img, wgt)
    landed(img_late.at[every, pl.ds(0, late_rows // down)], load_sem.at[6])
    landed(wgt_late, load_sem.at[7])

    def send_chunk(c):
        pl.loop(0, tiles - 1)(send_of(c, img_late, wgt_late))
        fill(tiles - 1, c, in_buf, me, img_late, wgt_late)

    pl.loop(1, chunks)(send_chunk)

    def place_of(t):
        for slot in range(cap):
            place = dst_ref[0, 0, slot, t]
            for j in range(blocks):
                is_here = (1 - jnp.minimum(jnp.abs(place - j), 1)).astype(jnp.float32)
                places[t, slot * blocks + j] = is_here

    repeat(tiles, place_of)

    @pl.when(not_first)
    def _():
        halo_down.wait_recv()

    @pl.when(not_last)
    def _():
        halo_up.wait_recv()

    row = lax.broadcasted_iota(jnp.int32, (HALO, LANES), 0)

    def halo_terms(n, steps):
        none = jnp.zeros((HALO, LANES), jnp.float32)
        columns = [
            halo[n, :, c * side : (c + 1) * side].astype(jnp.float32) for c in range(across)
        ]
        for c in range(across):
            left = columns[c - 1] if c > 0 else none
            right = columns[c + 1] if c < across - 1 else none
            moved = shifts(left, columns[c], right)
            total = none
            for a, step, kept in steps:
                part = taps[5 * a] * moved[0]
                for b in range(1, 5):
                    part = part + taps[5 * a + b] * moved[b]
                total = total + jnp.where(kept, pltpu.roll(part, step, 0), 0.0)
            yield c, total

    if down > 2:
        for at in range(across, (down - 1) * across):
            cor[at] = jnp.zeros(cor.shape[1:], cor.dtype)
    for c, total in halo_terms(0, ((0, 2, row < 2), (1, 1, row < 1))):
        cor[c] = total * wgt[c, :16].astype(jnp.float32)[:HALO]
    for c, total in halo_terms(1, ((4, 6, row >= 6), (3, 7, row >= 7))):
        at = (down - 1) * across + c
        total = total * wgt_late[at, -16:].astype(jnp.float32)[16 - HALO :]
        cor[at] = total if down > 1 else cor[at] + total

    def fill_cor(k, ref, place):
        target = owner(k)
        terms = [cor[src_ref[0, 0, slot, target]] * live(target, slot) for slot in range(cap)]
        ref[place] = jnp.concatenate(terms, 0).astype(jnp.bfloat16)

    def send_cor(k):
        fill_cor(k, out_cor, owner(k))
        cor_copy(k).start()

    pl.loop(0, tiles - 1)(send_cor)
    fill_cor(tiles - 1, in_cor, me)

    @pl.when((sec == 0) & not_first)
    def _():
        landed(pre.at[low_chunks, low_blocks], strip_recv.at[0])
        landed(pre.at[chunks - 1, pl.ds(0, 2)], strip_recv.at[1])
        for p in range(pairs):
            rim_anchor[p * CHUNK : (p + 1) * CHUNK] = packed_rim(pre, p)
        rim_anchor[rim_rows:] = jnp.zeros((HALO, side), rim_anchor.dtype)
        anchor_rim.start()

    def summed(part):
        totals = [None] * blocks
        for t in range(tiles):
            for slot in range(cap):
                value = part(t, slot).astype(jnp.float32)
                for j in range(blocks):
                    term = value * places[t, slot * blocks + j]
                    totals[j] = term if totals[j] is None else totals[j] + term
        return [total.astype(jnp.bfloat16) for total in totals]

    def gather_chunk(c):
        landed(in_buf.at[c, others], block_recv.at[c])
        for j, value in enumerate(summed(lambda t, slot: in_buf[c, t, slot])):
            strip[c, j] = value

    def start_rim(first, count):
        own, following = rim_copies(first, count)

        @pl.when(has_next & not_first)
        def _():
            following.start()

        @pl.when(not_first)
        def _():
            own.start()

    def send_rim(p):
        rim_out[p * CHUNK : (p + 1) * CHUNK] = packed_rim(strip, p)
        start_rim(p * CHUNK, CHUNK)

    for c in range(chunks - 1):
        gather_chunk(c)

        @pl.when(has_next)
        def _():
            onward(c).start()

        if c % 2 == 1:
            send_rim(c // 2)

    landed(in_cor.at[others], cor_recv)
    cors = [in_cor[t].astype(jnp.float32) for t in range(tiles)]
    for j, value in enumerate(summed(lambda t, slot: cors[t][slot * HALO : (slot + 1) * HALO])):
        strip_cor[j] = value
        if j == 0:
            rim_out[rim_rows:] = value
    start_rim(rim_rows, HALO)

    @pl.when(has_next)
    def _():
        onward_cor.start()

    gather_chunk(chunks - 1)
    send_rim(pairs - 1)

    @pl.when(has_next)
    def _():
        repeat(groups, lambda k: onward_last(groups - 1 - k).start())

    table_load.wait()
    right_table = tab.at[pl.ds(0, 2 * side)]
    left_table = tab.at[pl.ds(2 * side, 2 * half), pl.ds(0, side)]
    inverse_table = tab.at[pl.ds(2 * side + 2 * half, side)]

    def whole(ref, cor_ref, m):
        parts = [ref[c, m] for c in range(chunks)]
        parts[0], parts[-1] = mended(parts[0], parts[-1], cor_ref[m].astype(jnp.float32))
        return jnp.concatenate(parts, 0)

    def over_rows(block):
        return jnp.dot(left_table[...], block, preferred_element_type=jnp.float32)

    def spread_group(ref, cor_ref, g):
        pair = jnp.concatenate([whole(ref, cor_ref, 2 * g), whole(ref, cor_ref, 2 * g + 1)], 1)
        both = over_rows(pair)
        spread[2 * g], spread[2 * g + 1] = both[:, :side], both[:, side:]

    def spread_rim(ref):
        spread[blocks] = over_rows(jnp.concatenate([ref[c, blocks] for c in range(chunks)], 0))

    lane = lax.broadcasted_iota(jnp.int32, (half, side), 1)

    def spectra(g):
        rows = []
        for n in range(2):
            block, after = spread[2 * g + n], spread[2 * g + n + 1]
            parts = [(block[:half], after[:half]), (block[half:], after[half:])]
            rows.append(jnp.concatenate([here for here, _ in parts], 1))
            rows.append(
                jnp.concatenate([jnp.where(lane < side // 2, then, here) for here, then in parts], 1)
            )
        rows = jnp.concatenate(rows, 0).astype(jnp.bfloat16)
        return jnp.dot(rows, right_table[...], preferred_element_type=jnp.float32)

    def keep(g):
        spec[g] = spectra(g)

    repeat(groups, lambda g: spread_group(strip, strip_cor, g))
    repeat(groups - 1, keep)

    @pl.when(not_last)
    def _():
        landed(rim_own, own_recv)
        unpack_rim(rim_own, strip)

    spread_rim(strip)
    keep(groups - 1)

    @pl.when(has_prev | (me == 0))
    def _():
        landed(pre.at[low_chunks, low_blocks], strip_recv.at[0])

    @pl.when(has_prev)
    def _():
        landed(pre_cor, strip_cor_recv)

    @pl.when(not_last)
    def _():
        landed(rim_pre, next_recv)
        unpack_rim(rim_pre, pre)

    spread_rim(pre)

    row = lax.broadcasted_iota(jnp.int32, (8, side), 0)
    ends = jnp.where(row < 1, 1.0, 2.0)

    def correlate(k):
        g = groups - 1 - k

        @pl.when(has_prev | (me == 0) | (g > 0))
        def _():
            landed(pre.at[chunks - 1, pl.ds(2 * g, 2)], strip_recv.at[1 + g])

        spread_group(pre, pre_cor, g)
        earlier, current = spectra(g), spec.at[g]
        whitened = []
        for n in range(4):
            at = slice(n * half, (n + 1) * half)
            cur_re, cur_im = current[at, :side], current[at, side:]
            pre_re, pre_im = earlier[at, :side], earlier[at, side:]
            cross_re = cur_re * pre_re + cur_im * pre_im
            cross_im = cur_re * pre_im - cur_im * pre_re
            mag = jnp.sqrt(cross_re * cross_re + cross_im * cross_im)
            inner = mag[8:16]
            for low in range(16, half - 8, 8):
                inner = inner + mag[low : low + 8]
            total = 2.0 * inner + ends * (mag[:8] + mag[half - 8 :])
            mean = jnp.sum(total) * (1.0 / (side * side))
            scale = 1.0 / (mag + (0.1 * mean + 1e-06))
            whitened.append(jnp.concatenate([cross_re * scale, cross_im * scale], 1))
        whitened = jnp.concatenate(whitened, 0).astype(jnp.bfloat16)
        rows = jnp.dot(whitened, right_table[...], preferred_element_type=jnp.float32)
        for n in range(2):
            stacked = []
            for w in range(2):
                part = rows[(2 * n + w) * half : (2 * n + w + 1) * half]
                stacked.append(jnp.concatenate([part[:, :side], part[:, side:]], 0))
            stacked = jnp.concatenate(stacked, 1).astype(jnp.bfloat16)
            result = jnp.dot(
                inverse_table[...][:, : 2 * half], stacked, preferred_element_type=jnp.float32
            )
            out[0, 4 * g + 2 * n] = result[:, :side]
            out[0, 4 * g + 2 * n + 1] = result[:, side:]

    repeat(groups, correlate)

    @pl.when(not_last)
    def _():
        halo_down.wait_send()

    @pl.when(not_first)
    def _():
        halo_up.wait_send()
        landed(rim_out, own_send)

    @pl.when(has_next)
    def _():
        landed(strip.at[:, low_blocks], strip_send)
        onward_cor.wait_send()

    @pl.when((sec == 0) & not_first)
    def _():
        anchor_rim.wait_send()

    @pl.when(has_next & not_first)
    def _():
        landed(rim_out, next_send)

    landed(out_buf.at[:, others], block_send)
    landed(out_cor.at[others], cor_send)


def solution(mesh):
    sections, tiles = mesh.shape["sec"], mesh.shape["tile"]

    def body(image, weight, lens_filter_taps, block_src, block_dst, valid_count, anchor):
        th, tw = image.shape[1:]
        blocks, side = anchor.shape[:2]
        cap = block_src.shape[-1]
        anywhere = pl.BlockSpec(memory_space=pl.ANY)
        bf16 = jnp.bfloat16
        dma = pltpu.SemaphoreType.DMA
        across, down = tw // side, th // side
        chunks, half = side // CHUNK, side // 2 + 8
        pairs = chunks // 2
        tables = dft_tables(side)
        return pl.pallas_call(
            functools.partial(kernel, sections, tiles),
            out_shape=pltpu.VMEM((1, 2 * blocks, side, side), jnp.float32),
            in_specs=[anywhere] * 8,
            out_specs=pl.BlockSpec(memory_space=pltpu.VMEM),
            scratch_shapes=[
                pltpu.SMEM(lens_filter_taps.shape, jnp.float32),
                pltpu.SMEM((1, 1, cap, tiles), jnp.int32),
                pltpu.SMEM((1, 1, cap, tiles), jnp.int32),
                pltpu.SMEM(valid_count.shape, jnp.int32),
                pltpu.VMEM((down * (across + 2), CHUNK + 2 * EDGE, side), bf16),
                pltpu.VMEM((down * (across + 2), side - CHUNK + 2 * EDGE, side), bf16),
                pltpu.VMEM((down * across, CHUNK, side), bf16),
                pltpu.VMEM((down * across, side - CHUNK, side), bf16),
                pltpu.VMEM((2, HALO, tw), bf16),
                pltpu.VMEM((down * across, HALO, side), jnp.float32),
                pltpu.VMEM((chunks, tiles, cap, CHUNK, side), bf16),
                pltpu.VMEM((chunks, tiles, cap, CHUNK, side), bf16),
                pltpu.VMEM((tiles, cap * HALO, side), bf16),
                pltpu.VMEM((tiles, cap * HALO, side), bf16),
                pltpu.VMEM((chunks, blocks + 1, CHUNK, side), bf16),
                pltpu.VMEM((chunks, blocks + 1, CHUNK, side), bf16),
                pltpu.VMEM((blocks, HALO, side), bf16),
                pltpu.VMEM((blocks, HALO, side), bf16),
                pltpu.VMEM((pairs * CHUNK + HALO, side), bf16),
                pltpu.VMEM((pairs * CHUNK + HALO, side), bf16),
                pltpu.VMEM((pairs * CHUNK + HALO, side), bf16),
                pltpu.VMEM((pairs * CHUNK + HALO, side), bf16),
                pltpu.VMEM((blocks + 1, 2 * half, side), jnp.float32),
                pltpu.VMEM((blocks // 2, 4 * half, 2 * side), jnp.float32),
                pltpu.VMEM(tables.shape, bf16),
                pltpu.SMEM((tiles, cap * blocks), jnp.float32),
                dma((9,)),
                dma((2,)),
                dma((2,)),
                dma((chunks,)),
                dma((1 + blocks // 2,)),
                dma((7,)),
                dma((4,)),
            ],
            compiler_params=pltpu.CompilerParams(collective_id=0, has_side_effects=True),
        )(
            image,
            weight,
            anchor,
            tables,
            lens_filter_taps,
            block_src.transpose(0, 1, 3, 2),
            block_dst.transpose(0, 2, 3, 1),
            valid_count,
        )

    in_specs = (
        P("sec", "tile", None),
        P("sec", "tile", None),
        P("sec", "tile", None),
        P("sec", "tile", None, None),
        P("sec", None, "tile", None),
        P("sec", "tile", None),
        P("tile", None, None),
    )
    out_specs = P("sec", "tile", None, None)
    return jax.shard_map(body, mesh=mesh, in_specs=in_specs, out_specs=out_specs, check_vma=False)
```
